768 devices in a mesh: ep: 32 (over y, x), grp: 24 (over z, core).
Axes of the slice: x: 4, y: 8, z: 12, core: 2. Of those that a mesh axis runs over, the one named last changes fastest.
Arguments:
- token_inputs: bfloat16 [98304, 768], P(('ep', 'grp')), may hold values from -6 to 6
- output_grads: bfloat16 [98304, 768], P(('ep', 'grp')), may hold values from -6 to 6
- gate_probs: float32 [98304], P(('ep', 'grp')), may hold values from 0.2 to 1
- token_slots: int32 [98304], replicated, may hold values from 0 to 767, as said below
- slot_experts: int32 [32, 24], P('ep'), may hold values from 0 to 127, as said below
- slot_capacity: int32 [32, 24], P('ep', 'grp'), may hold values from 64 to 256, as said below
- weight_in: bfloat16 [32, 24, 768, 1024], P('ep', 'grp'), as said below
- weight_out: bfloat16 [32, 24, 768, 1024], P('ep', 'grp'), as said below
Outputs:
- input_grads: bfloat16 [98304, 768], P(('ep', 'grp'))
- expert_grads: bfloat16 [2, 128, 768, 1024], P(None, 'ep', 'grp')
The draws below stay inside these ranges and needn't reach their ends.
Inputs may be any that keep to these rules, and one draw needn't show every extreme that they name: `token_slots`: tokens stand in blocks of 128, one block for each device in the order ep then grp. Of one block's tokens at most 8 go to slots of one grp index; for every ep index, one grp index takes exactly 8 from every block of that ep index. Of the tokens of all blocks of one ep index bound for one grp index, at most 8 go to any one slot, and exactly 8 in some cases. `slot_experts`: the 24 slots of ep index c host experts c * 4 to c * 4 + 3, each on 1 to 8 slots, and one of them in every column on exactly 8 slots. `slot_capacity`: some slot has capacity 256. `weight_in`: the copies on all slots that host one expert are equal. `weight_out`: the copies on all slots that host one expert are equal.
All inputs are finite; a program needn't handle non-finite values.
Results may differ from the reference program's by a relative error of at most 0.0064.
Values may be sent and summed in bfloat16 or wider, within the bound.
No kernel may reach another device: no remote copies, remote signals or barrier semaphores. Data moves between devices by JAX's collectives and lax.ppermute only.
A program may use at most 32 MiB of HBM per device.

```python
import jax
import jax.numpy as jnp
from jax import lax

D = 768
FF = 1024
EXP_COL = 4
TOK_DEV = 128
EP_SIZE = 32
GRP_SIZE = 24
SLOTS = 768
TOKENS = 98304
EXPERTS = 128
CAP_MAX = 256
ROW_CAP = 8
COL_CAP = 8


def expert_layout(key):
    key_list = jax.random.split(key, 4)
    biggest = min(8, GRP_SIZE - EXP_COL + 1)
    extra = GRP_SIZE - biggest - (EXP_COL - 1)
    first_extra = jax.random.randint(key_list[0], (EP_SIZE,), max(0, extra - 14), min(7, extra) + 1)
    remain = extra - first_extra
    second_extra = jax.random.randint(key_list[1], (EP_SIZE,), jnp.maximum(0, remain - 7), jnp.minimum(7, remain) + 1)
    third_extra = remain - second_extra
    part_sizes = jnp.stack([jnp.full((EP_SIZE,), biggest, jnp.int32), first_extra + 1, second_extra + 1, third_extra + 1], axis=1).astype(jnp.int32)
    shuffle_scores = jax.random.randint(key_list[2], (EP_SIZE, EXP_COL), 0, 1 << 16) * EXP_COL + jnp.arange(EXP_COL, dtype=jnp.int32)[None, :]
    part_sizes = jnp.take_along_axis(part_sizes, jnp.argsort(shuffle_scores, axis=1), axis=1)
    bounds = jnp.cumsum(part_sizes, axis=1)
    positions = jnp.arange(GRP_SIZE, dtype=jnp.int32)
    local_label = jnp.sum((positions[None, :, None] >= bounds[:, None, :]).astype(jnp.int32), axis=2)
    row_scores = jax.random.randint(key_list[3], (EP_SIZE, GRP_SIZE), 0, 1 << 16) * GRP_SIZE + positions[None, :]
    row_perm = jnp.argsort(row_scores, axis=1)
    placed = jnp.take_along_axis(local_label, jnp.argsort(row_perm, axis=1), axis=1)
    return (placed + jnp.arange(EP_SIZE, dtype=jnp.int32)[:, None] * EXP_COL).astype(jnp.int32)


def draw_slot_experts(key, part):
    return expert_layout(jax.random.fold_in(key, 7))


def expert_copies(key, salt, fan_in):
    layout = expert_layout(jax.random.fold_in(key, 7)).reshape(-1)
    weight_key = jax.random.fold_in(key, salt)
    table = jax.random.normal(weight_key, (EXPERTS, D, FF), jnp.float32) * fan_in ** (-0.5)
    table = table.astype(jnp.bfloat16)
    return table[layout].reshape(EP_SIZE, GRP_SIZE, D, FF)


def draw_weight_in(key, part):
    return expert_copies(key, 101, D)


def draw_weight_out(key, part):
    return expert_copies(key, 102, FF)


def draw_slot_capacity(key, part):
    key_list = jax.random.split(jax.random.fold_in(key, 9), 2)
    capacity = jax.random.randint(key_list[0], (SLOTS,), TOK_DEV // 2, CAP_MAX + 1)
    chosen = jax.random.randint(key_list[1], (), 0, SLOTS)
    capacity = jnp.where(jnp.arange(SLOTS, dtype=jnp.int32) == chosen, CAP_MAX, capacity)
    return capacity.reshape(EP_SIZE, GRP_SIZE).astype(jnp.int32)


def draw_token_slots(key, part):
    key_list = jax.random.split(jax.random.fold_in(key, 13), 6)
    pool_len = (GRP_SIZE - 1) * ROW_CAP
    hot_row = jax.random.randint(key_list[0], (EP_SIZE,), 0, GRP_SIZE)
    source_ep = jnp.arange(SLOTS, dtype=jnp.int32) // GRP_SIZE
    source_hot = hot_row[source_ep]
    base_rows = jnp.arange(pool_len, dtype=jnp.int32) // ROW_CAP
    row_pool = base_rows[None, :] + (base_rows[None, :] >= source_hot[:, None]).astype(jnp.int32)
    pool_scores = jax.random.randint(key_list[1], (SLOTS, pool_len), 0, 1 << 16) * pool_len + jnp.arange(pool_len, dtype=jnp.int32)[None, :]
    row_pool = jnp.take_along_axis(row_pool, jnp.argsort(pool_scores, axis=1), axis=1)
    dest_rows = jnp.concatenate([jnp.broadcast_to(source_hot[:, None], (SLOTS, ROW_CAP)), row_pool[:, :TOK_DEV - ROW_CAP]], axis=1)
    token_scores = jax.random.randint(key_list[2], (SLOTS, TOK_DEV), 0, 1 << 16) * TOK_DEV + jnp.arange(TOK_DEV, dtype=jnp.int32)[None, :]
    dest_rows = jnp.take_along_axis(dest_rows, jnp.argsort(token_scores, axis=1), axis=1).reshape(-1)
    mid_ids = jnp.repeat(source_ep, TOK_DEV) * GRP_SIZE + dest_rows
    shuffle = jax.random.permutation(key_list[3], TOKENS).astype(jnp.int32)
    sorted_order = jnp.argsort(mid_ids * TOKENS + shuffle)
    sorted_mid = mid_ids[sorted_order]
    counts = jnp.zeros((SLOTS,), jnp.int32).at[mid_ids].add(1)
    starts = jnp.cumsum(counts).astype(jnp.int32) - counts
    mid_rank = jnp.arange(TOKENS, dtype=jnp.int32) - starts[sorted_mid]
    hot_col = jax.random.randint(key_list[4], (GRP_SIZE,), 0, EP_SIZE)
    mid_hot = hot_col[sorted_mid % GRP_SIZE]
    table_len = (EP_SIZE - 1) * COL_CAP
    base_cols = jnp.arange(table_len, dtype=jnp.int32) // COL_CAP
    table_scores = jax.random.randint(key_list[5], (SLOTS, table_len), 0, 1 << 16) * table_len + jnp.arange(table_len, dtype=jnp.int32)[None, :]
    col_table = base_cols[jnp.argsort(table_scores, axis=1)]
    pick_index = jnp.clip(mid_rank - COL_CAP, 0, table_len - 1)
    other_cols = col_table[sorted_mid, pick_index]
    other_cols = other_cols + (other_cols >= mid_hot).astype(jnp.int32)
    sorted_cols = jnp.where(mid_rank < COL_CAP, mid_hot, other_cols)
    dest_cols = jnp.zeros((TOKENS,), jnp.int32).at[sorted_order].set(sorted_cols)
    return (dest_cols * GRP_SIZE + dest_rows).astype(jnp.int32)


def levels(own_key, extent, cuts, smallest, top_value):
    def one(dim, parts):
        heights = jax.random.uniform(jax.random.fold_in(jax.random.fold_in(own_key, 6), dim), (parts,), jnp.float32, smallest / len(cuts), top_value / len(cuts))
        return jnp.repeat(jnp.exp(heights), extent[dim] // parts).reshape((-1,) + (1,) * (len(extent) - dim - 1))

    gain = one(*cuts[0])
    for cut in cuts[1:]:
        gain = gain * one(*cut)
    return gain


def scatter_about(own_key, extent, scale, most, cuts=(), kind=jnp.bfloat16):
    gain = levels(own_key, extent, cuts, -0.22, 0.18) if cuts else 1.0
    drawn = jax.random.normal(own_key, extent, jnp.float32) * scale * gain
    return jnp.minimum(jnp.maximum(drawn, -most), most).astype(kind)


def setup_inputs(seed: int = 0) -> dict:
    splits = jax.random.split(jax.random.key(seed), 9)
    return {
        "token_inputs": scatter_about(splits[0], (TOKENS, D), 1.0, 6.0, ((0, 768),)),
        "output_grads": scatter_about(splits[1], (TOKENS, D), 1.0, 6.0, ((0, 768),)),
        "gate_probs": jnp.clip(0.2 + 0.8 * jax.random.uniform(splits[2], (TOKENS,), jnp.float32) ** levels(splits[2], (TOKENS,), ((0, 768),), -0.2, 0.2), 0.2, 1.0),
        "token_slots": draw_token_slots(jax.random.fold_in(splits[8], 71), 0),
        "slot_experts": draw_slot_experts(jax.random.fold_in(splits[8], 71), 0),
        "slot_capacity": draw_slot_capacity(jax.random.fold_in(splits[8], 71), 0),
        "weight_in": draw_weight_in(jax.random.fold_in(splits[8], 71), 0),
        "weight_out": draw_weight_out(jax.random.fold_in(splits[8], 71), 0),
    }


coef_a = 0.7978845608028654
coef_b = 0.044715


def gelu_pair(preact):
    square = preact * preact
    tanh_value = jnp.tanh(coef_a * preact * (1.0 + coef_b * square))
    half_sum = 0.5 * (1.0 + tanh_value)
    gelu_value = preact * half_sum
    gelu_slope = half_sum + 0.5 * preact * (1.0 - tanh_value * tanh_value) * coef_a * (1.0 + 3.0 * coef_b * square)
    return gelu_value, gelu_slope


def slot_block(input_rows, grad_rows, first_weight, second_weight):
    preact = jnp.dot(input_rows, first_weight, preferred_element_type=jnp.float32)
    gelu_value, gelu_slope = gelu_pair(preact)
    activated = gelu_value.astype(jnp.bfloat16)
    hidden_grad = jnp.dot(grad_rows, second_weight, preferred_element_type=jnp.float32)
    preact_grad = (hidden_grad * gelu_slope).astype(jnp.bfloat16)
    row_grads = lax.dot_general(preact_grad, first_weight, (((1,), (1,)), ((), ())), preferred_element_type=jnp.float32).astype(jnp.bfloat16)
    grad_in = lax.dot_general(input_rows, preact_grad, (((0,), (0,)), ((), ())), preferred_element_type=jnp.float32)
    grad_out = lax.dot_general(grad_rows, activated, (((0,), (0,)), ((), ())), preferred_element_type=jnp.float32)
    return row_grads, grad_in, grad_out


def reference(token_inputs, output_grads, gate_probs, token_slots, slot_experts, slot_capacity, weight_in, weight_out):
    scaled = (gate_probs[:, None] * output_grads.astype(jnp.float32)).astype(jnp.bfloat16)
    token_ids = jnp.arange(TOKENS, dtype=jnp.int32)
    sorted_order = jnp.argsort(token_slots * TOKENS + token_ids).astype(jnp.int32)
    sorted_slots = token_slots[sorted_order]
    counts = jnp.zeros((SLOTS,), jnp.int32).at[token_slots].add(1)
    starts = jnp.cumsum(counts).astype(jnp.int32) - counts
    slot_rank = token_ids - starts[sorted_slots]
    capacity = slot_capacity.reshape(SLOTS)
    kept_mask = slot_rank < capacity[sorted_slots]
    row_table = jnp.full((SLOTS, CAP_MAX), TOKENS, jnp.int32)
    row_table = row_table.at[sorted_slots, jnp.where(kept_mask, slot_rank, CAP_MAX)].set(sorted_order, mode="drop")
    slot_loads = jnp.minimum(counts, capacity)
    inputs_padded = jnp.concatenate([token_inputs, jnp.zeros((1, D), jnp.bfloat16)], axis=0)
    scaled_padded = jnp.concatenate([scaled, jnp.zeros((1, D), jnp.bfloat16)], axis=0)
    block_rows = min(128, CAP_MAX)
    block_count = CAP_MAX // block_rows
    weights_first = weight_in.reshape(SLOTS, D, FF)
    weights_second = weight_out.reshape(SLOTS, D, FF)
    experts_flat = slot_experts.reshape(SLOTS)

    def column_work(column):
        def row_step(carry, row_id):
            slot_id = column * GRP_SIZE + row_id
            first_weight = weights_first[slot_id]
            second_weight = weights_second[slot_id]

            def block_step(inner_sums, block_id):
                take_index = lax.dynamic_slice_in_dim(row_table[slot_id], block_id * block_rows, block_rows)

                def active_block(unused):
                    return slot_block(inputs_padded[take_index], scaled_padded[take_index], first_weight, second_weight)

                def spare_block(unused):
                    return (jnp.zeros((block_rows, D), jnp.bfloat16), jnp.zeros((D, FF), jnp.float32), jnp.zeros((D, FF), jnp.float32))

                row_grads, grad_in, grad_out = lax.cond(block_id * block_rows < slot_loads[slot_id], active_block, spare_block, 0)
                return (inner_sums[0] + grad_in, inner_sums[1] + grad_out), row_grads

            zero_grad = jnp.zeros((D, FF), jnp.float32)
            grad_sums, row_grads = lax.scan(block_step, (zero_grad, zero_grad), jnp.arange(block_count, dtype=jnp.int32))
            local_expert = experts_flat[slot_id] - column * EXP_COL
            member = (jnp.arange(EXP_COL, dtype=jnp.int32) == local_expert).astype(jnp.float32)
            both_grads = lax.optimization_barrier(jnp.stack([grad_sums[0], grad_sums[1]]).astype(jnp.bfloat16)).astype(jnp.float32)
            carry = carry + member[None, :, None, None] * both_grads[:, None]
            return carry, row_grads.reshape(CAP_MAX, D)

        start_sums = jnp.zeros((2, EXP_COL, D, FF), jnp.float32)
        column_sums, column_rows = lax.scan(row_step, start_sums, jnp.arange(GRP_SIZE, dtype=jnp.int32))
        return column_sums.astype(jnp.bfloat16), column_rows

    all_sums, all_rows = lax.map(column_work, jnp.arange(EP_SIZE, dtype=jnp.int32))
    expert_grads = jnp.transpose(all_sums, (1, 0, 2, 3, 4)).reshape(2, EXPERTS, D, FF)
    input_grads = jnp.zeros((TOKENS + 1, D), jnp.bfloat16).at[row_table.reshape(-1)].set(all_rows.reshape(-1, D))
    return input_grads[:TOKENS], expert_grads
```

```python
import jax
import jax.numpy as jnp
from jax import lax
from jax.experimental import pallas as pl
from jax.experimental.pallas import tpu as pltpu
from jax.sharding import PartitionSpec as P

EP = 32
GRP = 24
Z = 12
EXP_COL = 4
TOK = 128
CAP = 8
D = 768
FF = 1024
ROWS_MID = GRP * CAP
ROWS_SLOT = EP * CAP
FEAT = D // GRP

coef_a = 0.7978845608028654
coef_b = 0.044715

f32 = jnp.float32
bf16 = jnp.bfloat16
i32 = jnp.int32


def iota(shape, dim):
    return lax.broadcasted_iota(i32, shape, dim)


def split_slot(slots):
    col = (slots * 2731) >> 16
    return col, slots - col * GRP


def to_column(row):
    n = row.shape[1]
    eye = iota((n, n), 0) == iota((n, n), 1)
    return jnp.sum(jnp.where(eye, jnp.broadcast_to(row, (n, n)), 0.0), axis=1, keepdims=True)


def to_row(column):
    n = column.shape[0]
    eye = iota((n, n), 0) == iota((n, n), 1)
    return jnp.sum(jnp.where(eye, jnp.broadcast_to(column, (n, n)), 0.0), axis=0, keepdims=True)


def earlier_equal(row):
    n = row.shape[1]
    same = to_column(row) == row
    before = iota((n, n), 0) < iota((n, n), 1)
    return jnp.sum(jnp.where(same & before, 1.0, 0.0), axis=0, keepdims=True)


def send_kernel(place_ref, slots_ref, inputs_ref, grads_ref, gate_ref, rows_ref, pick_ref):
    own = place_ref[0] * GRP + place_ref[1]
    slots = slots_ref[pl.ds(own % 8, 1), :]
    dest = split_slot(slots)[1].astype(f32)
    spot = dest * CAP + earlier_equal(dest)
    pick = (iota((ROWS_MID, TOK), 0).astype(f32) == spot).astype(bf16)
    pick_ref[...] = pick
    scaled = (to_column(gate_ref[...]) * grads_ref[...].astype(f32)).astype(bf16)
    rows_ref[:, :D] = jnp.dot(pick, inputs_ref[...], preferred_element_type=f32).astype(bf16)
    rows_ref[:, D:] = jnp.dot(pick, scaled, preferred_element_type=f32).astype(bf16)


def route_kernel(place_ref, block_ref, slots_ref, capacity_ref, forward_ref, kept_ref, wide_ref):
    grp_index = place_ref[1]
    col, row = split_slot(block_ref[...])
    hit = jnp.where(row == grp_index, 1.0, 0.0)
    upper = (iota((TOK, TOK), 0) < iota((TOK, TOK), 1)).astype(bf16)
    spot = jnp.dot(hit.astype(bf16), upper, preferred_element_type=f32)
    value = hit * (col + 1).astype(f32)
    lane = iota((CAP, TOK), 0).astype(f32)
    for s in range(GRP):
        wide_ref[s * CAP : (s + 1) * CAP, :] = jnp.where(
            spot[s : s + 1, :] == lane, jnp.broadcast_to(value[s : s + 1, :], (CAP, TOK)), 0.0
        )
    dest = to_row(jnp.sum(wide_ref[...], axis=1, keepdims=True))
    target = jnp.where(dest > 0.0, (dest - 1.0) * CAP + earlier_equal(dest), -1.0)
    forward_ref[...] = (iota((ROWS_SLOT, ROWS_MID), 0).astype(f32) == target).astype(bf16)
    my_slot = place_ref[0] * GRP + grp_index
    arrived = jnp.concatenate(
        [
            jnp.sum(
                jnp.where(slots_ref[e * GRP : (e + 1) * GRP, :] == my_slot, 1.0, 0.0),
                axis=0,
                keepdims=True,
            )
            for e in range(EP)
        ],
        axis=0,
    ).astype(bf16)
    counts = jnp.dot(arrived, jnp.ones((TOK, TOK), bf16), preferred_element_type=f32)
    lower = (iota((EP, EP), 1) < iota((EP, EP), 0)).astype(bf16)
    starts = jnp.dot(lower, counts.astype(bf16), preferred_element_type=f32)
    capacity = capacity_ref[0].astype(f32)
    for e in range(EP):
        kept = (lane < counts[e : e + 1, :]) & (starts[e : e + 1, :] + lane < capacity)
        kept_ref[e * CAP : (e + 1) * CAP, :] = jnp.where(kept, 1.0, 0.0)


def forward_kernel(forward_ref, rows_ref, out_ref):
    out_ref[...] = jnp.dot(forward_ref[...], rows_ref[...], preferred_element_type=f32).astype(bf16)


def back_kernel(pick_ref, rows_ref, out_ref):
    out_ref[...] = lax.dot_general(
        pick_ref[...], rows_ref[...], (((0,), (0,)), ((), ())), preferred_element_type=f32
    ).astype(bf16)


def gelu_pair(preact):
    square = preact * preact
    tanh_value = jnp.tanh(coef_a * preact * (1.0 + coef_b * square))
    half_sum = 0.5 * (1.0 + tanh_value)
    gelu_value = preact * half_sum
    gelu_slope = half_sum + 0.5 * preact * (1.0 - tanh_value * tanh_value) * coef_a * (
        1.0 + 3.0 * coef_b * square
    )
    return gelu_value, gelu_slope


def slot_kernel(
    place_ref, rows_ref, kept_ref, first_ref, second_ref, back_ref, mine_ref, other_ref, grad_ref
):
    core = place_ref[1] % 2
    kept = kept_ref[:, 0:1] > 0.0
    inputs = jnp.where(kept, rows_ref[:, :D].astype(f32), 0.0).astype(bf16)
    grads = jnp.where(kept, rows_ref[:, D:].astype(f32), 0.0).astype(bf16)
    preact = jnp.dot(inputs, first_ref[...], preferred_element_type=f32)
    hidden_grad = jnp.dot(grads, second_ref[...], preferred_element_type=f32)
    gelu_value, gelu_slope = gelu_pair(preact)
    activated = gelu_value.astype(bf16)
    preact_grad = (hidden_grad * gelu_slope).astype(bf16)
    for k, (left, right) in enumerate(((inputs, preact_grad), (grads, activated))):
        grad_ref[...] = lax.dot_general(
            left, right, (((0,), (0,)), ((), ())), preferred_element_type=f32
        ).astype(bf16)
        for z in range(Z):
            start = z * 2 * FEAT
            mine = pl.multiple_of(start + core * FEAT, FEAT)
            other = pl.multiple_of(start + (1 - core) * FEAT, FEAT)
            mine_ref[z, k] = grad_ref[pl.ds(mine, FEAT), :]
            other_ref[z, k] = grad_ref[pl.ds(other, FEAT), :]
    back_ref[...] = lax.dot_general(
        preact_grad, first_ref[...], (((1,), (1,)), ((), ())), preferred_element_type=f32
    ).astype(bf16)


def merge_kernel(owner_ref, mine_ref, partner_ref, out_ref):
    for k in range(2):
        mine = mine_ref[0, k].astype(f32)
        partner = partner_ref[0, k].astype(f32)
        for e in range(EXP_COL):
            first = jnp.where(owner_ref[0] == e, mine, 0.0)
            second = jnp.where(owner_ref[1] == e, partner, 0.0)
            out_ref[0, k, e] = (first + second).astype(bf16)


def shape(dims, dtype=bf16):
    return jax.ShapeDtypeStruct(dims, dtype)


def whole():
    return pl.BlockSpec(memory_space=pltpu.VMEM)


def scalars():
    return pl.BlockSpec(memory_space=pltpu.SMEM)


def per_device(
    token_inputs,
    output_grads,
    gate_probs,
    token_slots,
    slot_experts,
    slot_capacity,
    weight_in,
    weight_out,
):
    ep_index = lax.axis_index("ep")
    grp_index = lax.axis_index("grp")
    place = jnp.stack([ep_index, grp_index]).astype(i32)
    slots = token_slots.reshape(EP * GRP, TOK)

    rows_out, pick = pl.pallas_call(
        send_kernel,
        grid_spec=pltpu.PrefetchScalarGridSpec(
            num_scalar_prefetch=1,
            grid=(1,),
            in_specs=[
                pl.BlockSpec((8, TOK), lambda i, p: ((p[0] * GRP + p[1]) // 8, 0)),
                pl.BlockSpec((TOK, D), lambda i, p: (0, 0)),
                pl.BlockSpec((TOK, D), lambda i, p: (0, 0)),
                pl.BlockSpec((1, TOK), lambda i, p: (0, 0)),
            ],
            out_specs=[
                pl.BlockSpec((ROWS_MID, 2 * D), lambda i, p: (0, 0)),
                pl.BlockSpec((ROWS_MID, TOK), lambda i, p: (0, 0)),
            ],
        ),
        out_shape=[shape((ROWS_MID, 2 * D)), shape((ROWS_MID, TOK))],
        name="send",
    )(place, slots, token_inputs, output_grads, gate_probs.reshape(1, TOK))
    rows_mid = lax.all_to_all(
        rows_out.reshape(GRP, CAP, 2 * D), "grp", split_axis=0, concat_axis=0, tiled=True
    ).reshape(ROWS_MID, 2 * D)

    forward, kept = pl.pallas_call(
        route_kernel,
        grid_spec=pltpu.PrefetchScalarGridSpec(
            num_scalar_prefetch=1,
            grid=(1,),
            in_specs=[
                pl.BlockSpec((GRP, TOK), lambda i, p: (p[0], 0)),
                pl.BlockSpec((EP * GRP, TOK), lambda i, p: (0, 0)),
                pl.BlockSpec(memory_space=pltpu.SMEM),
            ],
            out_specs=[
                pl.BlockSpec((ROWS_SLOT, ROWS_MID), lambda i, p: (0, 0)),
                pl.BlockSpec((ROWS_SLOT, TOK), lambda i, p: (0, 0)),
            ],
            scratch_shapes=[pltpu.VMEM((ROWS_MID, TOK), f32)],
        ),
        out_shape=[shape((ROWS_SLOT, ROWS_MID)), shape((ROWS_SLOT, TOK), f32)],
        name="route",
    )(place, slots, slots, slot_capacity.reshape(1))

    rows_fwd = pl.pallas_call(
        forward_kernel,
        in_specs=[whole(), whole()],
        out_specs=whole(),
        out_shape=shape((ROWS_SLOT, 2 * D)),
        name="forward",
    )(forward, rows_mid)
    rows_slot = lax.all_to_all(
        rows_fwd.reshape(EP, CAP, 2 * D), "ep", split_axis=0, concat_axis=0, tiled=True
    ).reshape(ROWS_SLOT, 2 * D)

    back_rows, mine, other = pl.pallas_call(
        slot_kernel,
        in_specs=[scalars()] + [whole()] * 4,
        out_specs=[whole()] * 3,
        out_shape=[
            shape((ROWS_SLOT, D)),
            shape((Z, 2, FEAT, FF)),
            shape((Z, 2, FEAT, FF)),
        ],
        scratch_shapes=[pltpu.VMEM((D, FF), bf16)],
        name="slot",
    )(place, rows_slot, kept, weight_in.reshape(D, FF), weight_out.reshape(D, FF))

    partner = lax.ppermute(other, "grp", [(g, g ^ 1) for g in range(GRP)])
    experts = slot_experts.reshape(GRP) - ep_index * EXP_COL
    owners = lax.dynamic_slice_in_dim(experts, (grp_index // 2) * 2, 2)
    owners = jnp.where(grp_index % 2 == 0, owners, owners[::-1])
    merged = pl.pallas_call(
        merge_kernel,
        grid_spec=pltpu.PrefetchScalarGridSpec(
            num_scalar_prefetch=1,
            grid=(Z,),
            in_specs=[pl.BlockSpec((1, 2, FEAT, FF), lambda i, p: (i, 0, 0, 0))] * 2,
            out_specs=pl.BlockSpec((1, 2, EXP_COL, FEAT, FF), lambda i, p: (i, 0, 0, 0, 0)),
        ),
        out_shape=shape((Z, 2, EXP_COL, FEAT, FF)),
        name="merge",
    )(owners, mine, partner)
    expert_grads = lax.psum_scatter(
        merged.reshape(Z * 2 * EXP_COL * FEAT, FF),
        "grp",
        scatter_dimension=0,
        tiled=True,
        axis_index_groups=[[2 * z + c for z in range(Z)] for c in range(2)],
    ).reshape(2, EXP_COL, FEAT, FF)

    mid_back = lax.all_to_all(
        back_rows.reshape(EP, CAP, D), "ep", split_axis=0, concat_axis=0, tiled=True
    ).reshape(ROWS_SLOT, D)
    source_back = pl.pallas_call(
        back_kernel,
        in_specs=[whole(), whole()],
        out_specs=whole(),
        out_shape=shape((ROWS_MID, D)),
        name="back_mid",
    )(forward, mid_back)
    own_back = lax.all_to_all(
        source_back.reshape(GRP, CAP, D), "grp", split_axis=0, concat_axis=0, tiled=True
    ).reshape(ROWS_MID, D)
    input_grads = pl.pallas_call(
        back_kernel,
        in_specs=[whole(), whole()],
        out_specs=whole(),
        out_shape=shape((TOK, D)),
        name="back_own",
    )(pick, own_back)
    return input_grads, expert_grads


def solution(mesh):
    in_specs = (
        P(("ep", "grp"), None),
        P(("ep", "grp"), None),
        P(("ep", "grp")),
        P(),
        P("ep", None),
        P("ep", "grp"),
        P("ep", "grp", None, None),
        P("ep", "grp", None, None),
    )
    out_specs = (P(("ep", "grp"), None), P(None, "ep", "grp", None))
    return jax.shard_map(
        per_device, mesh=mesh, in_specs=in_specs, out_specs=out_specs, check_vma=False
    )
```

```python
import jax
import jax.numpy as jnp
from jax import lax
from jax.experimental import pallas as pl
from jax.experimental.pallas import tpu as pltpu
from jax.sharding import PartitionSpec as P

EP = 32
GRP = 24
Z = 12
EXP_COL = 4
TOK = 128
CAP = 8
D = 768
FF = 1024
ROWS_MID = GRP * CAP
ROWS_SLOT = EP * CAP
FEAT = D // GRP

coef_a = 0.7978845608028654
coef_b = 0.044715

f32 = jnp.float32
bf16 = jnp.bfloat16
i32 = jnp.int32


def iota(shape, dim):
    return lax.broadcasted_iota(i32, shape, dim)


def split_slot(slots):
    col = (slots * 2731) >> 16
    return col, slots - col * GRP


def to_column(row):
    n = row.shape[1]
    eye = iota((n, n), 0) == iota((n, n), 1)
    return jnp.sum(jnp.where(eye, jnp.broadcast_to(row, (n, n)), 0.0), axis=1, keepdims=True)


def to_row(column):
    n = column.shape[0]
    eye = iota((n, n), 0) == iota((n, n), 1)
    return jnp.sum(jnp.where(eye, jnp.broadcast_to(column, (n, n)), 0.0), axis=0, keepdims=True)


def earlier_equal(row):
    n = row.shape[1]
    same = to_column(row) == row
    before = iota((n, n), 0) < iota((n, n), 1)
    return jnp.sum(jnp.where(same & before, 1.0, 0.0), axis=0, keepdims=True)


def send_kernel(
    slots_hbm, inputs_hbm, grads_hbm, gate_hbm, rows_hbm, pick_ref,
    slots_ref, inputs_ref, grads_ref, gate_ref, left_ref, right_ref, sems
):
    own = lax.axis_index("ep") * GRP + lax.axis_index("grp")
    tile = pl.multiple_of((own // 8) * 8, 8)
    loads = [
        pltpu.make_async_copy(source, target, sems.at[k])
        for k, (source, target) in enumerate(
            (
                (slots_hbm.at[pl.ds(tile, 8)], slots_ref),
                (inputs_hbm, inputs_ref),
                (gate_hbm, gate_ref),
                (grads_hbm, grads_ref),
            )
        )
    ]
    for load in loads:
        load.start()
    loads[0].wait()
    slots = slots_ref[pl.ds(own % 8, 1), :]
    dest = split_slot(slots)[1].astype(f32)
    spot = dest * CAP + earlier_equal(dest)
    pick = (iota((ROWS_MID, TOK), 0).astype(f32) == spot).astype(bf16)
    pick_ref[...] = pick
    loads[1].wait()
    left_ref[...] = jnp.dot(pick, inputs_ref[...], preferred_element_type=f32).astype(bf16)
    left = pltpu.make_async_copy(left_ref, rows_hbm.at[:, pl.ds(0, D)], sems.at[4])
    left.start()
    loads[2].wait()
    loads[3].wait()
    scaled = (to_column(gate_ref[...]) * grads_ref[...].astype(f32)).astype(bf16)
    right_ref[...] = jnp.dot(pick, scaled, preferred_element_type=f32).astype(bf16)
    right = pltpu.make_async_copy(right_ref, rows_hbm.at[:, pl.ds(D, D)], sems.at[5])
    right.start()
    left.wait()
    right.wait()


def route_kernel(
    place_ref, block_ref, slots_ref, capacity_ref, forward_ref, kept_ref, blank_hbm,
    wide_ref, zero_ref, sem
):
    zero_ref[...] = jnp.zeros_like(zero_ref)
    fills = [pltpu.make_async_copy(zero_ref, blank_hbm.at[z], sem.at[z]) for z in range(Z)]
    for fill in fills:
        fill.start()
    grp_index = place_ref[1]
    col, row = split_slot(block_ref[...])
    hit = jnp.where(row == grp_index, 1.0, 0.0)
    upper = (iota((TOK, TOK), 0) < iota((TOK, TOK), 1)).astype(bf16)
    spot = jnp.dot(hit.astype(bf16), upper, preferred_element_type=f32)
    value = hit * (col + 1).astype(f32)
    lane = iota((CAP, TOK), 0).astype(f32)
    for s in range(GRP):
        wide_ref[s * CAP : (s + 1) * CAP, :] = jnp.where(
            spot[s : s + 1, :] == lane, jnp.broadcast_to(value[s : s + 1, :], (CAP, TOK)), 0.0
        )
    dest = to_row(jnp.sum(wide_ref[...], axis=1, keepdims=True))
    target = jnp.where(dest > 0.0, (dest - 1.0) * CAP + earlier_equal(dest), -1.0)
    forward_ref[...] = (iota((ROWS_SLOT, ROWS_MID), 0).astype(f32) == target).astype(bf16)
    my_slot = place_ref[0] * GRP + grp_index
    arrived = jnp.concatenate(
        [
            jnp.sum(
                jnp.where(slots_ref[e * GRP : (e + 1) * GRP, :] == my_slot, 1.0, 0.0),
                axis=0,
                keepdims=True,
            )
            for e in range(EP)
        ],
        axis=0,
    ).astype(bf16)
    counts = jnp.dot(arrived, jnp.ones((TOK, TOK), bf16), preferred_element_type=f32)
    lower = (iota((EP, EP), 1) < iota((EP, EP), 0)).astype(bf16)
    starts = jnp.dot(lower, counts.astype(bf16), preferred_element_type=f32)
    capacity = capacity_ref[0, 0].astype(f32)
    for e in range(EP):
        kept = (lane < counts[e : e + 1, :]) & (starts[e : e + 1, :] + lane < capacity)
        kept_ref[e * CAP : (e + 1) * CAP, :] = jnp.where(kept, 1.0, 0.0)
    for fill in fills:
        fill.wait()


def back_kernel(pick_ref, rows_ref, out_ref):
    out_ref[...] = lax.dot_general(
        pick_ref[...], rows_ref[...], (((0,), (0,)), ((), ())), preferred_element_type=f32
    ).astype(bf16)


def gelu_pair(preact):
    square = preact * preact
    tanh_value = jnp.tanh(coef_a * preact * (1.0 + coef_b * square))
    half_sum = 0.5 * (1.0 + tanh_value)
    gelu_value = preact * half_sum
    gelu_slope = half_sum + 0.5 * preact * (1.0 - tanh_value * tanh_value) * coef_a * (
        1.0 + 3.0 * coef_b * square
    )
    return gelu_value, gelu_slope


def slot_kernel(
    experts_ref, rows_hbm, kept_hbm, first_hbm, second_hbm, blank_hbm,
    back_ref, merged_hbm, mine_hbm, other_hbm,
    rows_ref, kept_ref, first_ref, second_ref, grad_refs, sems
):
    grp_index = lax.axis_index("grp")
    core = grp_index % 2
    expert = experts_ref[0, grp_index] - lax.axis_index("ep") * EXP_COL
    loads = [
        pltpu.make_async_copy(source, target, sems.at[k])
        for k, (source, target) in enumerate(
            (
                (rows_hbm, rows_ref),
                (kept_hbm, kept_ref),
                (first_hbm, first_ref),
                (second_hbm, second_ref),
            )
        )
    ]
    for load in loads:
        load.start()
    loads[0].wait()
    loads[1].wait()
    kept = kept_ref[:, 0:1] > 0.0
    inputs = jnp.where(kept, rows_ref[:, :D].astype(f32), 0.0).astype(bf16)
    grads = jnp.where(kept, rows_ref[:, D:].astype(f32), 0.0).astype(bf16)

    def store(k, left, right):
        grad = lax.dot_general(left, right, (((0,), (0,)), ((), ())), preferred_element_type=f32)
        grad_refs[k] = grad.astype(bf16).reshape(Z, 2, FEAT, FF)
        copies = (
            pltpu.make_async_copy(
                grad_refs.at[k, :, 1 - core], other_hbm.at[:, k], sems.at[4 + 3 * k]
            ),
            pltpu.make_async_copy(
                grad_refs.at[k, :, core], merged_hbm.at[:, k, expert], sems.at[5 + 3 * k]
            ),
            pltpu.make_async_copy(
                grad_refs.at[k, :, core], mine_hbm.at[:, k], sems.at[6 + 3 * k]
            ),
        )
        for copy in copies:
            copy.start()
        return copies

    loads[2].wait()
    preact = jnp.dot(inputs, first_ref[...], preferred_element_type=f32)
    gelu_value, gelu_slope = gelu_pair(preact)
    stores = store(1, grads, gelu_value.astype(bf16))
    loads[3].wait()
    hidden_grad = jnp.dot(grads, second_ref[...], preferred_element_type=f32)
    preact_grad = (hidden_grad * gelu_slope).astype(bf16)
    stores += store(0, inputs, preact_grad)
    back_ref[...] = lax.dot_general(
        preact_grad, first_ref[...], (((1,), (1,)), ((), ())), preferred_element_type=f32
    ).astype(bf16)
    for copy in stores:
        copy.wait()


def shape(dims, dtype=bf16):
    return jax.ShapeDtypeStruct(dims, dtype)


def whole():
    return pl.BlockSpec(memory_space=pltpu.VMEM)


def scalars():
    return pl.BlockSpec(memory_space=pltpu.SMEM)


def anywhere():
    return pl.BlockSpec(memory_space=pl.ANY)


def per_device(
    token_inputs,
    output_grads,
    gate_probs,
    token_slots,
    slot_experts,
    slot_capacity,
    weight_in,
    weight_out,
):
    ep_index = lax.axis_index("ep")
    grp_index = lax.axis_index("grp")
    place = jnp.stack([ep_index, grp_index]).astype(i32)
    slots = token_slots.reshape(EP * GRP, TOK)

    rows_out, pick = pl.pallas_call(
        send_kernel,
        in_specs=[anywhere()] * 4,
        out_specs=[anywhere(), whole()],
        out_shape=[shape((ROWS_MID, 2 * D)), shape((ROWS_MID, TOK))],
        scratch_shapes=[
            pltpu.VMEM((8, TOK), i32),
            pltpu.VMEM((TOK, D), bf16),
            pltpu.VMEM((TOK, D), bf16),
            pltpu.VMEM((1, TOK), f32),
            pltpu.VMEM((ROWS_MID, D), bf16),
            pltpu.VMEM((ROWS_MID, D), bf16),
            pltpu.SemaphoreType.DMA((6,)),
        ],
        name="send",
    )(slots, token_inputs, output_grads, gate_probs.reshape(1, TOK))
    rows_mid = lax.all_to_all(
        rows_out.reshape(GRP, CAP, 2 * D), "grp", split_axis=0, concat_axis=0, tiled=True
    ).reshape(ROWS_MID, 2 * D)

    forward, kept, blank = pl.pallas_call(
        route_kernel,
        grid_spec=pltpu.PrefetchScalarGridSpec(
            num_scalar_prefetch=1,
            grid=(1,),
            in_specs=[
                pl.BlockSpec((GRP, TOK), lambda i, p: (p[0], 0)),
                pl.BlockSpec((EP * GRP, TOK), lambda i, p: (0, 0)),
                pl.BlockSpec(memory_space=pltpu.SMEM),
            ],
            out_specs=[
                pl.BlockSpec((ROWS_SLOT, ROWS_MID), lambda i, p: (0, 0)),
                pl.BlockSpec((ROWS_SLOT, TOK), lambda i, p: (0, 0)),
                anywhere(),
            ],
            scratch_shapes=[
                pltpu.VMEM((ROWS_MID, TOK), f32),
                pltpu.VMEM((2, EXP_COL, FEAT, FF), bf16),
                pltpu.SemaphoreType.DMA((Z,)),
            ],
        ),
        out_shape=[
            shape((ROWS_SLOT, ROWS_MID)),
            shape((ROWS_SLOT, TOK), f32),
            shape((Z, 2, EXP_COL, FEAT, FF)),
        ],
        name="route",
    )(place, slots, slots, slot_capacity)

    rows_fwd = jnp.dot(forward, rows_mid, preferred_element_type=f32).astype(bf16)
    rows_slot = lax.all_to_all(
        rows_fwd.reshape(EP, CAP, 2 * D), "ep", split_axis=0, concat_axis=0, tiled=True
    ).reshape(ROWS_SLOT, 2 * D)

    back_rows, merged, mine, other = pl.pallas_call(
        slot_kernel,
        in_specs=[scalars()] + [anywhere()] * 5,
        out_specs=[whole(), anywhere(), anywhere(), anywhere()],
        out_shape=[
            shape((ROWS_SLOT, D)),
            shape((Z, 2, EXP_COL, FEAT, FF)),
            shape((Z, 2, FEAT, FF)),
            shape((Z, 2, FEAT, FF)),
        ],
        scratch_shapes=[
            pltpu.VMEM((ROWS_SLOT, 2 * D), bf16),
            pltpu.VMEM((ROWS_SLOT, TOK), f32),
            pltpu.VMEM((D, FF), bf16),
            pltpu.VMEM((D, FF), bf16),
            pltpu.VMEM((2, Z, 2, FEAT, FF), bf16),
            pltpu.SemaphoreType.DMA((10,)),
        ],
        input_output_aliases={5: 1},
        name="slot",
    )(
        slot_experts,
        rows_slot,
        kept,
        weight_in.reshape(D, FF),
        weight_out.reshape(D, FF),
        blank,
    )

    partner = lax.ppermute(other, "grp", [(g, g ^ 1) for g in range(GRP)])
    experts = slot_experts.reshape(GRP)
    mine_expert = lax.dynamic_index_in_dim(experts, grp_index, keepdims=False)
    partner_expert = lax.dynamic_index_in_dim(
        experts, grp_index + 1 - 2 * (grp_index % 2), keepdims=False
    )
    local = partner_expert - ep_index * EXP_COL
    total = partner.astype(f32) + jnp.where(mine_expert == partner_expert, mine.astype(f32), 0.0)
    merged = lax.dynamic_update_index_in_dim(merged, total.astype(bf16), local, axis=2)
    expert_grads = lax.psum_scatter(
        merged.reshape(Z * 2 * EXP_COL * FEAT, FF),
        "grp",
        scatter_dimension=0,
        tiled=True,
        axis_index_groups=[[2 * z + c for z in range(Z)] for c in range(2)],
    ).reshape(2, EXP_COL, FEAT, FF)

    mid_back = lax.all_to_all(
        back_rows.reshape(EP, CAP, D), "ep", split_axis=0, concat_axis=0, tiled=True
    ).reshape(ROWS_SLOT, D)
    source_back = pl.pallas_call(
        back_kernel,
        in_specs=[whole(), whole()],
        out_specs=whole(),
        out_shape=shape((ROWS_MID, D)),
        name="back_mid",
    )(forward, mid_back)
    own_back = lax.all_to_all(
        source_back.reshape(GRP, CAP, D), "grp", split_axis=0, concat_axis=0, tiled=True
    ).reshape(ROWS_MID, D)
    input_grads = pl.pallas_call(
        back_kernel,
        in_specs=[whole(), whole()],
        out_specs=whole(),
        out_shape=shape((TOK, D)),
        name="back_own",
    )(pick, own_back)
    return input_grads, expert_grads


def solution(mesh):
    in_specs = (
        P(("ep", "grp"), None),
        P(("ep", "grp"), None),
        P(("ep", "grp")),
        P(),
        P("ep", None),
        P("ep", "grp"),
        P("ep", "grp", None, None),
        P("ep", "grp", None, None),
    )
    out_specs = (P(("ep", "grp"), None), P(None, "ep", "grp", None))
    return jax.shard_map(
        per_device, mesh=mesh, in_specs=in_specs, out_specs=out_specs, check_vma=False
    )
```

```python
import jax
import jax.numpy as jnp
from jax import lax
from jax.experimental import pallas as pl
from jax.experimental.pallas import tpu as pltpu
from jax.sharding import PartitionSpec as P

EP = 32
GRP = 24
Z = 12
EXP_COL = 4
TOK = 128
CAP = 8
D = 768
FF = 1024
ROWS_MID = GRP * CAP
ROWS_SLOT = EP * CAP
FEAT = D // GRP

coef_a = 0.7978845608028654
coef_b = 0.044715

f32 = jnp.float32
bf16 = jnp.bfloat16
i32 = jnp.int32


def iota(shape, dim):
    return lax.broadcasted_iota(i32, shape, dim)


def split_slot(slots):
    col = (slots * 2731) >> 16
    return col, slots - col * GRP


def to_column(row):
    n = row.shape[1]
    eye = iota((n, n), 0) == iota((n, n), 1)
    return jnp.sum(jnp.where(eye, jnp.broadcast_to(row, (n, n)), 0.0), axis=1, keepdims=True)


def to_row(column):
    n = column.shape[0]
    eye = iota((n, n), 0) == iota((n, n), 1)
    return jnp.sum(jnp.where(eye, jnp.broadcast_to(column, (n, n)), 0.0), axis=0, keepdims=True)


def earlier_equal(row):
    n = row.shape[1]
    same = to_column(row) == row
    before = iota((n, n), 0) < iota((n, n), 1)
    return jnp.sum(jnp.where(same & before, 1.0, 0.0), axis=0, keepdims=True)


def send_kernel(
    slots_hbm, inputs_hbm, grads_hbm, gate_hbm, rows_hbm, pick_ref,
    slots_ref, inputs_ref, grads_ref, gate_ref, left_ref, right_ref, sems
):
    own = lax.axis_index("ep") * GRP + lax.axis_index("grp")
    tile = pl.multiple_of((own // 8) * 8, 8)
    loads = [
        pltpu.make_async_copy(source, target, sems.at[k])
        for k, (source, target) in enumerate(
            (
                (slots_hbm.at[pl.ds(tile, 8)], slots_ref),
                (inputs_hbm, inputs_ref),
                (gate_hbm, gate_ref),
                (grads_hbm, grads_ref),
            )
        )
    ]
    for load in loads:
        load.start()
    loads[0].wait()
    slots = slots_ref[pl.ds(own % 8, 1), :]
    dest = split_slot(slots)[1].astype(f32)
    spot = dest * CAP + earlier_equal(dest)
    pick = (iota((ROWS_MID, TOK), 0).astype(f32) == spot).astype(bf16)
    pick_ref[...] = pick
    loads[1].wait()
    left_ref[...] = jnp.dot(pick, inputs_ref[...], preferred_element_type=f32).astype(bf16)
    left = pltpu.make_async_copy(left_ref, rows_hbm.at[:, pl.ds(0, D)], sems.at[4])
    left.start()
    loads[2].wait()
    loads[3].wait()
    scaled = (to_column(gate_ref[...]) * grads_ref[...].astype(f32)).astype(bf16)
    right_ref[...] = jnp.dot(pick, scaled, preferred_element_type=f32).astype(bf16)
    right = pltpu.make_async_copy(right_ref, rows_hbm.at[:, pl.ds(D, D)], sems.at[5])
    right.start()
    left.wait()
    right.wait()


def route_kernel(
    place_ref, block_ref, slots_ref, capacity_ref, forward_ref, kept_ref, blank_hbm,
    wide_ref, zero_ref, sem
):
    zero_ref[...] = jnp.zeros_like(zero_ref)
    fills = [pltpu.make_async_copy(zero_ref, blank_hbm.at[z], sem.at[z]) for z in range(Z)]
    for fill in fills:
        fill.start()
    grp_index = place_ref[1]
    col, row = split_slot(block_ref[...])
    hit = jnp.where(row == grp_index, 1.0, 0.0)
    upper = (iota((TOK, TOK), 0) < iota((TOK, TOK), 1)).astype(bf16)
    spot = jnp.dot(hit.astype(bf16), upper, preferred_element_type=f32)
    value = hit * (col + 1).astype(f32)
    lane = iota((CAP, TOK), 0).astype(f32)
    for s in range(GRP):
        wide_ref[s * CAP : (s + 1) * CAP, :] = jnp.where(
            spot[s : s + 1, :] == lane, jnp.broadcast_to(value[s : s + 1, :], (CAP, TOK)), 0.0
        )
    dest = to_row(jnp.sum(wide_ref[...], axis=1, keepdims=True))
    target = jnp.where(dest > 0.0, (dest - 1.0) * CAP + earlier_equal(dest), -1.0)
    forward_ref[...] = (iota((ROWS_SLOT, ROWS_MID), 0).astype(f32) == target).astype(bf16)
    my_slot = place_ref[0] * GRP + grp_index
    arrived = jnp.concatenate(
        [
            jnp.sum(
                jnp.where(slots_ref[e * GRP : (e + 1) * GRP, :] == my_slot, 1.0, 0.0),
                axis=0,
                keepdims=True,
            )
            for e in range(EP)
        ],
        axis=0,
    ).astype(bf16)
    counts = jnp.dot(arrived, jnp.ones((TOK, TOK), bf16), preferred_element_type=f32)
    lower = (iota((EP, EP), 1) < iota((EP, EP), 0)).astype(bf16)
    starts = jnp.dot(lower, counts.astype(bf16), preferred_element_type=f32)
    capacity = capacity_ref[0, 0].astype(f32)
    for e in range(EP):
        kept = (lane < counts[e : e + 1, :]) & (starts[e : e + 1, :] + lane < capacity)
        kept_ref[e * CAP : (e + 1) * CAP, :] = jnp.where(kept, 1.0, 0.0)
    for fill in fills:
        fill.wait()


def back_kernel(pick_ref, rows_ref, out_ref):
    out_ref[...] = lax.dot_general(
        pick_ref[...], rows_ref[...], (((0,), (0,)), ((), ())), preferred_element_type=f32
    ).astype(bf16)


def gelu_pair(preact):
    square = preact * preact
    tanh_value = jnp.tanh(coef_a * preact * (1.0 + coef_b * square))
    half_sum = 0.5 * (1.0 + tanh_value)
    gelu_value = preact * half_sum
    gelu_slope = half_sum + 0.5 * preact * (1.0 - tanh_value * tanh_value) * coef_a * (
        1.0 + 3.0 * coef_b * square
    )
    return gelu_value, gelu_slope


def grad_kernel(
    experts_ref, rows_hbm, slope_hbm, act_hbm, other_rows_hbm, first_hbm, second_hbm, blank_hbm,
    merged_hbm,
    rows_ref, slope_ref, act_ref, other_rows_ref, first_ref, second_ref, across_ref, grad_ref,
    load_sems, store_sems
):
    grp_index = lax.axis_index("grp")
    core = grp_index % 2
    base = lax.axis_index("ep") * EXP_COL
    owners = (
        experts_ref[0, grp_index] - base,
        experts_ref[0, grp_index + 1 - 2 * core] - base,
    )
    loads = [
        pltpu.make_async_copy(source, target, load_sems.at[k])
        for k, (source, target) in enumerate(
            (
                (rows_hbm, rows_ref),
                (slope_hbm, slope_ref),
                (act_hbm, act_ref),
                (other_rows_hbm, other_rows_ref),
                (first_hbm, first_ref),
                (second_hbm, second_ref),
            )
        )
    ]
    for load in loads:
        load.start()

    def store(n, k):
        copy = pltpu.make_async_copy(
            grad_ref.at[n, k], merged_hbm.at[:, k, owners[n]], store_sems.at[n, k]
        )
        copy.start()
        return copy

    def halves(n, source):
        for k in range(2):
            across_ref[n, k] = source[:, k * D : (k + 1) * D].T.reshape(Z, 2, FEAT, ROWS_SLOT)
        return [across_ref[n, k, :, core].reshape(D // 2, ROWS_SLOT) for k in range(2)]

    loads[0].wait()
    lefts = halves(0, rows_ref)
    stores = []
    for k, source in enumerate((slope_ref, act_ref)):
        loads[1 + k].wait()
        grad = jnp.dot(lefts[k], source[...], preferred_element_type=f32)
        grad_ref[0, k] = grad.astype(bf16).reshape(Z, FEAT, FF)
        stores.append(store(0, k))
    loads[3].wait()
    loads[4].wait()
    preact = jnp.dot(other_rows_ref[:, :D], first_ref[...], preferred_element_type=f32)
    loads[5].wait()
    hidden_grad = jnp.dot(other_rows_ref[:, D:], second_ref[...], preferred_element_type=f32)
    lefts = halves(1, other_rows_ref)
    gelu_value, gelu_slope = gelu_pair(preact)
    rights = ((hidden_grad * gelu_slope).astype(bf16), gelu_value.astype(bf16))
    same = owners[0] == owners[1]
    for k in (1, 0):
        grad = jnp.dot(lefts[k], rights[k], preferred_element_type=f32)
        held = jnp.where(same, grad_ref[0, k].reshape(D // 2, FF).astype(f32), 0.0)
        grad_ref[1, k] = (grad + held).astype(bf16).reshape(Z, FEAT, FF)
        stores[k].wait()
        stores.append(store(1, k))
    stores[2].wait()
    stores[3].wait()


def shape(dims, dtype=bf16):
    return jax.ShapeDtypeStruct(dims, dtype)


def whole():
    return pl.BlockSpec(memory_space=pltpu.VMEM)


def scalars():
    return pl.BlockSpec(memory_space=pltpu.SMEM)


def anywhere():
    return pl.BlockSpec(memory_space=pl.ANY)


def per_device(
    token_inputs,
    output_grads,
    gate_probs,
    token_slots,
    slot_experts,
    slot_capacity,
    weight_in,
    weight_out,
):
    ep_index = lax.axis_index("ep")
    grp_index = lax.axis_index("grp")
    place = jnp.stack([ep_index, grp_index]).astype(i32)
    slots = token_slots.reshape(EP * GRP, TOK)

    rows_out, pick = pl.pallas_call(
        send_kernel,
        in_specs=[anywhere()] * 4,
        out_specs=[anywhere(), whole()],
        out_shape=[shape((ROWS_MID, 2 * D)), shape((ROWS_MID, TOK))],
        scratch_shapes=[
            pltpu.VMEM((8, TOK), i32),
            pltpu.VMEM((TOK, D), bf16),
            pltpu.VMEM((TOK, D), bf16),
            pltpu.VMEM((1, TOK), f32),
            pltpu.VMEM((ROWS_MID, D), bf16),
            pltpu.VMEM((ROWS_MID, D), bf16),
            pltpu.SemaphoreType.DMA((6,)),
        ],
        name="send",
    )(slots, token_inputs, output_grads, gate_probs.reshape(1, TOK))
    rows_mid = lax.all_to_all(
        rows_out.reshape(GRP, CAP, 2 * D), "grp", split_axis=0, concat_axis=0, tiled=True
    ).reshape(ROWS_MID, 2 * D)

    forward, kept, blank = pl.pallas_call(
        route_kernel,
        grid_spec=pltpu.PrefetchScalarGridSpec(
            num_scalar_prefetch=1,
            grid=(1,),
            in_specs=[
                pl.BlockSpec((GRP, TOK), lambda i, p: (p[0], 0)),
                pl.BlockSpec((EP * GRP, TOK), lambda i, p: (0, 0)),
                pl.BlockSpec(memory_space=pltpu.SMEM),
            ],
            out_specs=[
                pl.BlockSpec((ROWS_SLOT, ROWS_MID), lambda i, p: (0, 0)),
                pl.BlockSpec((ROWS_SLOT, TOK), lambda i, p: (0, 0)),
                anywhere(),
            ],
            scratch_shapes=[
                pltpu.VMEM((ROWS_MID, TOK), f32),
                pltpu.VMEM((2, EXP_COL, FEAT, FF), bf16),
                pltpu.SemaphoreType.DMA((Z,)),
            ],
        ),
        out_shape=[
            shape((ROWS_SLOT, ROWS_MID)),
            shape((ROWS_SLOT, TOK), f32),
            shape((Z, 2, EXP_COL, FEAT, FF)),
        ],
        name="route",
    )(place, slots, slots, slot_capacity)

    rows_fwd = jnp.dot(forward, rows_mid, preferred_element_type=f32).astype(bf16)
    rows_slot = lax.all_to_all(
        rows_fwd.reshape(EP, CAP, 2 * D), "ep", split_axis=0, concat_axis=0, tiled=True
    ).reshape(ROWS_SLOT, 2 * D)

    first = weight_in.reshape(D, FF)
    second = weight_out.reshape(D, FF)
    early_first, early_second, _ = lax.optimization_barrier((first, second, forward))
    swap = [(g, g ^ 1) for g in range(GRP)]
    other_first = lax.ppermute(early_first, "grp", swap)
    other_second = lax.ppermute(early_second, "grp", swap)
    rows_kept = jnp.where(kept[:, 0:1] > 0.0, rows_slot, jnp.zeros_like(rows_slot))
    other_rows = lax.ppermute(rows_kept, "grp", swap)
    preact = jnp.dot(rows_kept[:, :D], first, preferred_element_type=f32)
    gelu_value, gelu_slope = gelu_pair(preact)
    hidden_grad = jnp.dot(rows_kept[:, D:], second, preferred_element_type=f32)
    preact_grad = (hidden_grad * gelu_slope).astype(bf16)
    merged = pl.pallas_call(
        grad_kernel,
        in_specs=[scalars()] + [anywhere()] * 7,
        out_specs=anywhere(),
        out_shape=shape((Z, 2, EXP_COL, FEAT, FF)),
        scratch_shapes=[
            pltpu.VMEM((ROWS_SLOT, 2 * D), bf16),
            pltpu.VMEM((ROWS_SLOT, FF), bf16),
            pltpu.VMEM((ROWS_SLOT, FF), bf16),
            pltpu.VMEM((ROWS_SLOT, 2 * D), bf16),
            pltpu.VMEM((D, FF), bf16),
            pltpu.VMEM((D, FF), bf16),
            pltpu.VMEM((2, 2, Z, 2, FEAT, ROWS_SLOT), bf16),
            pltpu.VMEM((2, 2, Z, FEAT, FF), bf16),
            pltpu.SemaphoreType.DMA((6,)),
            pltpu.SemaphoreType.DMA((2, 2)),
        ],
        input_output_aliases={7: 0},
        name="grad",
    )(
        slot_experts,
        rows_kept,
        preact_grad,
        gelu_value.astype(bf16),
        other_rows,
        other_first,
        other_second,
        blank,
    )
    back_rows = lax.dot_general(
        preact_grad, first, (((1,), (1,)), ((), ())), preferred_element_type=f32
    ).astype(bf16)
    expert_grads = lax.psum_scatter(
        merged.reshape(Z * 2 * EXP_COL * FEAT, FF),
        "grp",
        scatter_dimension=0,
        tiled=True,
        axis_index_groups=[[2 * z + c for z in range(Z)] for c in range(2)],
    ).reshape(2, EXP_COL, FEAT, FF)

    mid_back = lax.all_to_all(
        back_rows.reshape(EP, CAP, D), "ep", split_axis=0, concat_axis=0, tiled=True
    ).reshape(ROWS_SLOT, D)
    source_back = pl.pallas_call(
        back_kernel,
        in_specs=[whole(), whole()],
        out_specs=whole(),
        out_shape=shape((ROWS_MID, D)),
        name="back_mid",
    )(forward, mid_back)
    own_back = lax.all_to_all(
        source_back.reshape(GRP, CAP, D), "grp", split_axis=0, concat_axis=0, tiled=True
    ).reshape(ROWS_MID, D)
    input_grads = pl.pallas_call(
        back_kernel,
        in_specs=[whole(), whole()],
        out_specs=whole(),
        out_shape=shape((TOK, D)),
        name="back_own",
    )(pick, own_back)
    return input_grads, expert_grads


def solution(mesh):
    in_specs = (
        P(("ep", "grp"), None),
        P(("ep", "grp"), None),
        P(("ep", "grp")),
        P(),
        P("ep", None),
        P("ep", "grp"),
        P("ep", "grp", None, None),
        P("ep", "grp", None, None),
    )
    out_specs = (P(("ep", "grp"), None), P(None, "ep", "grp", None))
    return jax.shard_map(
        per_device, mesh=mesh, in_specs=in_specs, out_specs=out_specs, check_vma=False
    )
```

```python
import jax
import jax.numpy as jnp
from jax import lax
from jax.experimental import pallas as pl
from jax.experimental.pallas import tpu as pltpu
from jax.sharding import PartitionSpec as P

EP = 32
GRP = 24
Z = 12
EXP_COL = 4
TOK = 128
CAP = 8
D = 768
FF = 1024
ROWS_MID = GRP * CAP
ROWS_SLOT = EP * CAP
FEAT = D // GRP

coef_a = 0.7978845608028654
coef_b = 0.044715

f32 = jnp.float32
bf16 = jnp.bfloat16
i32 = jnp.int32


def iota(shape, dim):
    return lax.broadcasted_iota(i32, shape, dim)


def split_slot(slots):
    col = (slots * 2731) >> 16
    return col, slots - col * GRP


def to_column(row):
    n = row.shape[1]
    eye = iota((n, n), 0) == iota((n, n), 1)
    return jnp.sum(jnp.where(eye, jnp.broadcast_to(row, (n, n)), 0.0), axis=1, keepdims=True)


def to_row(column):
    n = column.shape[0]
    eye = iota((n, n), 0) == iota((n, n), 1)
    return jnp.sum(jnp.where(eye, jnp.broadcast_to(column, (n, n)), 0.0), axis=0, keepdims=True)


def earlier_equal(row):
    n = row.shape[1]
    same = to_column(row) == row
    before = iota((n, n), 0) < iota((n, n), 1)
    return jnp.sum(jnp.where(same & before, 1.0, 0.0), axis=0, keepdims=True)


def send_kernel(
    slots_hbm, inputs_hbm, grads_hbm, gate_hbm, rows_hbm, pick_ref,
    slots_ref, inputs_ref, grads_ref, gate_ref, left_ref, right_ref, sems
):
    own = lax.axis_index("ep") * GRP + lax.axis_index("grp")
    tile = pl.multiple_of((own // 8) * 8, 8)
    loads = [
        pltpu.make_async_copy(source, target, sems.at[k])
        for k, (source, target) in enumerate(
            (
                (slots_hbm.at[pl.ds(tile, 8)], slots_ref),
                (inputs_hbm, inputs_ref),
                (gate_hbm, gate_ref),
                (grads_hbm, grads_ref),
            )
        )
    ]
    for load in loads:
        load.start()
    loads[0].wait()
    slots = slots_ref[pl.ds(own % 8, 1), :]
    dest = split_slot(slots)[1].astype(f32)
    spot = dest * CAP + earlier_equal(dest)
    pick = (iota((ROWS_MID, TOK), 0).astype(f32) == spot).astype(bf16)
    pick_ref[...] = pick
    loads[1].wait()
    left_ref[...] = jnp.dot(pick, inputs_ref[...], preferred_element_type=f32).astype(bf16)
    left = pltpu.make_async_copy(left_ref, rows_hbm.at[:, pl.ds(0, D)], sems.at[4])
    left.start()
    loads[2].wait()
    loads[3].wait()
    scaled = (to_column(gate_ref[...]) * grads_ref[...].astype(f32)).astype(bf16)
    right_ref[...] = jnp.dot(pick, scaled, preferred_element_type=f32).astype(bf16)
    right = pltpu.make_async_copy(right_ref, rows_hbm.at[:, pl.ds(D, D)], sems.at[5])
    right.start()
    left.wait()
    right.wait()


def route_kernel(
    place_ref, block_ref, slots_ref, capacity_ref, forward_ref, kept_ref, blank_hbm,
    wide_ref, zero_ref, sem
):
    zero_ref[...] = jnp.zeros_like(zero_ref)
    fills = [pltpu.make_async_copy(zero_ref, blank_hbm.at[z], sem.at[z]) for z in range(Z)]
    for fill in fills:
        fill.start()
    grp_index = place_ref[1]
    col, row = split_slot(block_ref[...])
    hit = jnp.where(row == grp_index, 1.0, 0.0)
    upper = (iota((TOK, TOK), 0) < iota((TOK, TOK), 1)).astype(bf16)
    spot = jnp.dot(hit.astype(bf16), upper, preferred_element_type=f32)
    value = hit * (col + 1).astype(f32)
    lane = iota((CAP, TOK), 0).astype(f32)
    for s in range(GRP):
        wide_ref[s * CAP : (s + 1) * CAP, :] = jnp.where(
            spot[s : s + 1, :] == lane, jnp.broadcast_to(value[s : s + 1, :], (CAP, TOK)), 0.0
        )
    dest = to_row(jnp.sum(wide_ref[...], axis=1, keepdims=True))
    target = jnp.where(dest > 0.0, (dest - 1.0) * CAP + earlier_equal(dest), -1.0)
    forward_ref[...] = (iota((ROWS_SLOT, ROWS_MID), 0).astype(f32) == target).astype(bf16)
    my_slot = place_ref[0] * GRP + grp_index
    arrived = jnp.concatenate(
        [
            jnp.sum(
                jnp.where(slots_ref[e * GRP : (e + 1) * GRP, :] == my_slot, 1.0, 0.0),
                axis=0,
                keepdims=True,
            )
            for e in range(EP)
        ],
        axis=0,
    ).astype(bf16)
    counts = jnp.dot(arrived, jnp.ones((TOK, TOK), bf16), preferred_element_type=f32)
    lower = (iota((EP, EP), 1) < iota((EP, EP), 0)).astype(bf16)
    starts = jnp.dot(lower, counts.astype(bf16), preferred_element_type=f32)
    capacity = capacity_ref[0, 0].astype(f32)
    for e in range(EP):
        kept = (lane < counts[e : e + 1, :]) & (starts[e : e + 1, :] + lane < capacity)
        kept_ref[e * CAP : (e + 1) * CAP, :] = jnp.where(kept, 1.0, 0.0)
    for fill in fills:
        fill.wait()


def back_kernel(pick_ref, rows_ref, out_ref):
    out_ref[...] = lax.dot_general(
        pick_ref[...], rows_ref[...], (((0,), (0,)), ((), ())), preferred_element_type=f32
    ).astype(bf16)


def gelu_pair(preact):
    square = preact * preact
    tanh_value = jnp.tanh(coef_a * preact * (1.0 + coef_b * square))
    half_sum = 0.5 * (1.0 + tanh_value)
    gelu_value = preact * half_sum
    gelu_slope = half_sum + 0.5 * preact * (1.0 - tanh_value * tanh_value) * coef_a * (
        1.0 + 3.0 * coef_b * square
    )
    return gelu_value, gelu_slope


def grad_kernel(
    experts_ref, rows_hbm, slope_hbm, act_hbm, other_rows_hbm, first_hbm, second_hbm, blank_hbm,
    merged_hbm,
    rows_ref, slope_ref, act_ref, other_rows_ref, first_ref, second_ref, across_ref, grad_ref,
    load_sems, store_sems
):
    grp_index = lax.axis_index("grp")
    core = grp_index % 2
    base = lax.axis_index("ep") * EXP_COL
    owners = (
        experts_ref[0, grp_index] - base,
        experts_ref[0, grp_index + 1 - 2 * core] - base,
    )
    loads = [
        pltpu.make_async_copy(source, target, load_sems.at[k])
        for k, (source, target) in enumerate(
            (
                (rows_hbm, rows_ref),
                (slope_hbm, slope_ref),
                (act_hbm, act_ref),
                (other_rows_hbm, other_rows_ref),
                (first_hbm, first_ref),
                (second_hbm, second_ref),
            )
        )
    ]
    for load in loads:
        load.start()

    def store(n, k):
        copy = pltpu.make_async_copy(
            grad_ref.at[n, k], merged_hbm.at[:, k, owners[n]], store_sems.at[n, k]
        )
        copy.start()
        return copy

    def halves(n, source):
        for k in range(2):
            across_ref[n, k] = source[:, k * D : (k + 1) * D].T.reshape(Z, 2, FEAT, ROWS_SLOT)
        return [across_ref[n, k, :, core].reshape(D // 2, ROWS_SLOT) for k in range(2)]

    loads[0].wait()
    lefts = halves(0, rows_ref)
    stores = []
    for k, source in enumerate((slope_ref, act_ref)):
        loads[1 + k].wait()
        grad = jnp.dot(lefts[k], source[...], preferred_element_type=f32)
        grad_ref[0, k] = grad.astype(bf16).reshape(Z, FEAT, FF)
        stores.append(store(0, k))
    loads[3].wait()
    loads[4].wait()
    preact = jnp.dot(other_rows_ref[:, :D], first_ref[...], preferred_element_type=f32)
    loads[5].wait()
    hidden_grad = jnp.dot(other_rows_ref[:, D:], second_ref[...], preferred_element_type=f32)
    lefts = halves(1, other_rows_ref)
    gelu_value, gelu_slope = gelu_pair(preact)
    rights = ((hidden_grad * gelu_slope).astype(bf16), gelu_value.astype(bf16))
    same = owners[0] == owners[1]
    for k in (1, 0):
        grad = jnp.dot(lefts[k], rights[k], preferred_element_type=f32)
        held = jnp.where(same, grad_ref[0, k].reshape(D // 2, FF).astype(f32), 0.0)
        grad_ref[1, k] = (grad + held).astype(bf16).reshape(Z, FEAT, FF)
        stores[k].wait()
        stores.append(store(1, k))
    stores[2].wait()
    stores[3].wait()


def shape(dims, dtype=bf16):
    return jax.ShapeDtypeStruct(dims, dtype)


def whole():
    return pl.BlockSpec(memory_space=pltpu.VMEM)


def scalars():
    return pl.BlockSpec(memory_space=pltpu.SMEM)


def anywhere():
    return pl.BlockSpec(memory_space=pl.ANY)


def per_device(
    token_inputs,
    output_grads,
    gate_probs,
    token_slots,
    slot_experts,
    slot_capacity,
    weight_in,
    weight_out,
):
    ep_index = lax.axis_index("ep")
    grp_index = lax.axis_index("grp")
    place = jnp.stack([ep_index, grp_index]).astype(i32)
    slots = token_slots.reshape(EP * GRP, TOK)

    rows_out, pick = pl.pallas_call(
        send_kernel,
        in_specs=[anywhere()] * 4,
        out_specs=[anywhere(), whole()],
        out_shape=[shape((ROWS_MID, 2 * D)), shape((ROWS_MID, TOK))],
        scratch_shapes=[
            pltpu.VMEM((8, TOK), i32),
            pltpu.VMEM((TOK, D), bf16),
            pltpu.VMEM((TOK, D), bf16),
            pltpu.VMEM((1, TOK), f32),
            pltpu.VMEM((ROWS_MID, D), bf16),
            pltpu.VMEM((ROWS_MID, D), bf16),
            pltpu.SemaphoreType.DMA((6,)),
        ],
        name="send",
    )(slots, token_inputs, output_grads, gate_probs.reshape(1, TOK))
    rows_mid = lax.all_to_all(
        rows_out.reshape(GRP, CAP, 2 * D), "grp", split_axis=0, concat_axis=0, tiled=True
    ).reshape(ROWS_MID, 2 * D)

    forward, kept, blank = pl.pallas_call(
        route_kernel,
        grid_spec=pltpu.PrefetchScalarGridSpec(
            num_scalar_prefetch=1,
            grid=(1,),
            in_specs=[
                pl.BlockSpec((GRP, TOK), lambda i, p: (p[0], 0)),
                pl.BlockSpec((EP * GRP, TOK), lambda i, p: (0, 0)),
                pl.BlockSpec(memory_space=pltpu.SMEM),
            ],
            out_specs=[
                pl.BlockSpec((ROWS_SLOT, ROWS_MID), lambda i, p: (0, 0)),
                pl.BlockSpec((ROWS_SLOT, TOK), lambda i, p: (0, 0)),
                anywhere(),
            ],
            scratch_shapes=[
                pltpu.VMEM((ROWS_MID, TOK), f32),
                pltpu.VMEM((2, EXP_COL, FEAT, FF), bf16),
                pltpu.SemaphoreType.DMA((Z,)),
            ],
        ),
        out_shape=[
            shape((ROWS_SLOT, ROWS_MID)),
            shape((ROWS_SLOT, TOK), f32),
            shape((Z, 2, EXP_COL, FEAT, FF)),
        ],
        name="route",
    )(place, slots, slots, slot_capacity)

    first = weight_in.reshape(D, FF)
    second = weight_out.reshape(D, FF)
    early_first, early_second, _ = lax.optimization_barrier((first, second, forward))
    swap = [(g, g ^ 1) for g in range(GRP)]
    other_first = lax.ppermute(early_first, "grp", swap)
    other_second = lax.ppermute(early_second, "grp", swap)
    rows_mid, other_first, other_second, kept_rows = lax.optimization_barrier(
        (rows_mid, other_first, other_second, kept[:, 0] > 0.0)
    )
    rows_fwd = jnp.dot(forward, rows_mid, preferred_element_type=f32).astype(bf16)
    rows_slot = lax.all_to_all(
        rows_fwd.reshape(EP, CAP, 2 * D), "ep", split_axis=0, concat_axis=0, tiled=True
    ).reshape(ROWS_SLOT, 2 * D)

    rows_kept = jnp.where(kept_rows[:, None], rows_slot, jnp.zeros_like(rows_slot))
    other_rows = lax.ppermute(rows_kept, "grp", swap)
    preact = jnp.dot(rows_kept[:, :D], first, preferred_element_type=f32)
    gelu_value, gelu_slope = gelu_pair(preact)
    hidden_grad = jnp.dot(rows_kept[:, D:], second, preferred_element_type=f32)
    preact_grad = (hidden_grad * gelu_slope).astype(bf16)
    merged = pl.pallas_call(
        grad_kernel,
        in_specs=[scalars()] + [anywhere()] * 7,
        out_specs=anywhere(),
        out_shape=shape((Z, 2, EXP_COL, FEAT, FF)),
        scratch_shapes=[
            pltpu.VMEM((ROWS_SLOT, 2 * D), bf16),
            pltpu.VMEM((ROWS_SLOT, FF), bf16),
            pltpu.VMEM((ROWS_SLOT, FF), bf16),
            pltpu.VMEM((ROWS_SLOT, 2 * D), bf16),
            pltpu.VMEM((D, FF), bf16),
            pltpu.VMEM((D, FF), bf16),
            pltpu.VMEM((2, 2, Z, 2, FEAT, ROWS_SLOT), bf16),
            pltpu.VMEM((2, 2, Z, FEAT, FF), bf16),
            pltpu.SemaphoreType.DMA((6,)),
            pltpu.SemaphoreType.DMA((2, 2)),
        ],
        input_output_aliases={7: 0},
        name="grad",
    )(
        slot_experts,
        rows_kept,
        preact_grad,
        gelu_value.astype(bf16),
        other_rows,
        other_first,
        other_second,
        blank,
    )
    back_rows = lax.dot_general(
        preact_grad, first, (((1,), (1,)), ((), ())), preferred_element_type=f32
    ).astype(bf16)
    expert_grads = lax.psum_scatter(
        merged.reshape(Z * 2 * EXP_COL * FEAT, FF),
        "grp",
        scatter_dimension=0,
        tiled=True,
        axis_index_groups=[[2 * z + c for z in range(Z)] for c in range(2)],
    ).reshape(2, EXP_COL, FEAT, FF)

    mid_back = lax.all_to_all(
        back_rows.reshape(EP, CAP, D), "ep", split_axis=0, concat_axis=0, tiled=True
    ).reshape(ROWS_SLOT, D)
    source_back = pl.pallas_call(
        back_kernel,
        in_specs=[whole(), whole()],
        out_specs=whole(),
        out_shape=shape((ROWS_MID, D)),
        name="back_mid",
    )(forward, mid_back)
    own_back = lax.all_to_all(
        source_back.reshape(GRP, CAP, D), "grp", split_axis=0, concat_axis=0, tiled=True
    ).reshape(ROWS_MID, D)
    input_grads = pl.pallas_call(
        back_kernel,
        in_specs=[whole(), whole()],
        out_specs=whole(),
        out_shape=shape((TOK, D)),
        name="back_own",
    )(pick, own_back)
    return input_grads, expert_grads


def solution(mesh):
    in_specs = (
        P(("ep", "grp"), None),
        P(("ep", "grp"), None),
        P(("ep", "grp")),
        P(),
        P("ep", None),
        P("ep", "grp"),
        P("ep", "grp", None, None),
        P("ep", "grp", None, None),
    )
    out_specs = (P(("ep", "grp"), None), P(None, "ep", "grp", None))
    return jax.shard_map(
        per_device, mesh=mesh, in_specs=in_specs, out_specs=out_specs, check_vma=False
    )
```

```python
import jax
import jax.numpy as jnp
from jax import lax
from jax.experimental import pallas as pl
from jax.experimental.pallas import tpu as pltpu
from jax.sharding import PartitionSpec as P

EP = 32
GRP = 24
Z = 12
EXP_COL = 4
TOK = 128
CAP = 8
D = 768
FF = 1024
ROWS_MID = GRP * CAP
ROWS_SLOT = EP * CAP
FEAT = D // GRP

coef_a = 0.7978845608028654
coef_b = 0.044715

f32 = jnp.float32
bf16 = jnp.bfloat16
i32 = jnp.int32


def iota(shape, dim):
    return lax.broadcasted_iota(i32, shape, dim)


def split_slot(slots):
    col = (slots * 2731) >> 16
    return col, slots - col * GRP


def to_column(row):
    n = row.shape[1]
    eye = iota((n, n), 0) == iota((n, n), 1)
    return jnp.sum(jnp.where(eye, jnp.broadcast_to(row, (n, n)), 0.0), axis=1, keepdims=True)


def to_row(column):
    n = column.shape[0]
    eye = iota((n, n), 0) == iota((n, n), 1)
    return jnp.sum(jnp.where(eye, jnp.broadcast_to(column, (n, n)), 0.0), axis=0, keepdims=True)


def earlier_equal(row):
    n = row.shape[1]
    same = to_column(row) == row
    before = iota((n, n), 0) < iota((n, n), 1)
    return jnp.sum(jnp.where(same & before, 1.0, 0.0), axis=0, keepdims=True)


def send_kernel(
    slots_hbm, inputs_hbm, grads_hbm, gate_hbm, rows_hbm, pick_ref,
    slots_ref, inputs_ref, grads_ref, gate_ref, left_ref, right_ref, sems
):
    own = lax.axis_index("ep") * GRP + lax.axis_index("grp")
    tile = pl.multiple_of((own // 8) * 8, 8)
    loads = [
        pltpu.make_async_copy(source, target, sems.at[k])
        for k, (source, target) in enumerate(
            (
                (slots_hbm.at[pl.ds(tile, 8)], slots_ref),
                (inputs_hbm, inputs_ref),
                (gate_hbm, gate_ref),
                (grads_hbm, grads_ref),
            )
        )
    ]
    for load in loads:
        load.start()
    loads[0].wait()
    slots = slots_ref[pl.ds(own % 8, 1), :]
    dest = split_slot(slots)[1].astype(f32)
    spot = dest * CAP + earlier_equal(dest)
    pick = (iota((ROWS_MID, TOK), 0).astype(f32) == spot).astype(bf16)
    pick_ref[...] = pick
    loads[1].wait()
    left_ref[...] = jnp.dot(pick, inputs_ref[...], preferred_element_type=f32).astype(bf16)
    left = pltpu.make_async_copy(left_ref, rows_hbm.at[:, pl.ds(0, D)], sems.at[4])
    left.start()
    loads[2].wait()
    loads[3].wait()
    scaled = (to_column(gate_ref[...]) * grads_ref[...].astype(f32)).astype(bf16)
    right_ref[...] = jnp.dot(pick, scaled, preferred_element_type=f32).astype(bf16)
    right = pltpu.make_async_copy(right_ref, rows_hbm.at[:, pl.ds(D, D)], sems.at[5])
    right.start()
    left.wait()
    right.wait()


def route_kernel(
    place_ref, block_ref, slots_ref, capacity_ref, forward_ref, kept_ref, blank_hbm,
    wide_ref, zero_ref, sem
):
    zero_ref[...] = jnp.zeros_like(zero_ref)
    fills = [pltpu.make_async_copy(zero_ref, blank_hbm.at[z], sem.at[z]) for z in range(Z)]
    for fill in fills:
        fill.start()
    grp_index = place_ref[1]
    col, row = split_slot(block_ref[...])
    hit = jnp.where(row == grp_index, 1.0, 0.0)
    upper = (iota((TOK, TOK), 0) < iota((TOK, TOK), 1)).astype(bf16)
    spot = jnp.dot(hit.astype(bf16), upper, preferred_element_type=f32)
    value = hit * (col + 1).astype(f32)
    lane = iota((CAP, TOK), 0).astype(f32)
    for s in range(GRP):
        wide_ref[s * CAP : (s + 1) * CAP, :] = jnp.where(
            spot[s : s + 1, :] == lane, jnp.broadcast_to(value[s : s + 1, :], (CAP, TOK)), 0.0
        )
    dest = to_row(jnp.sum(wide_ref[...], axis=1, keepdims=True))
    target = jnp.where(dest > 0.0, (dest - 1.0) * CAP + earlier_equal(dest), -1.0)
    forward_ref[...] = (iota((ROWS_SLOT, ROWS_MID), 0).astype(f32) == target).astype(bf16)
    my_slot = place_ref[0] * GRP + grp_index
    arrived = jnp.concatenate(
        [
            jnp.sum(
                jnp.where(slots_ref[e * GRP : (e + 1) * GRP, :] == my_slot, 1.0, 0.0),
                axis=0,
                keepdims=True,
            )
            for e in range(EP)
        ],
        axis=0,
    ).astype(bf16)
    counts = jnp.dot(arrived, jnp.ones((TOK, TOK), bf16), preferred_element_type=f32)
    lower = (iota((EP, EP), 1) < iota((EP, EP), 0)).astype(bf16)
    starts = jnp.dot(lower, counts.astype(bf16), preferred_element_type=f32)
    capacity = capacity_ref[0, 0].astype(f32)
    for e in range(EP):
        kept = (lane < counts[e : e + 1, :]) & (starts[e : e + 1, :] + lane < capacity)
        kept_ref[e * CAP : (e + 1) * CAP, :] = jnp.where(kept, 1.0, 0.0)
    for fill in fills:
        fill.wait()


def back_kernel(pick_ref, rows_ref, out_ref):
    out_ref[...] = lax.dot_general(
        pick_ref[...], rows_ref[...], (((0,), (0,)), ((), ())), preferred_element_type=f32
    ).astype(bf16)


def gelu_pair(preact):
    square = preact * preact
    tanh_value = jnp.tanh(coef_a * preact * (1.0 + coef_b * square))
    half_sum = 0.5 * (1.0 + tanh_value)
    gelu_value = preact * half_sum
    gelu_slope = half_sum + 0.5 * preact * (1.0 - tanh_value * tanh_value) * coef_a * (
        1.0 + 3.0 * coef_b * square
    )
    return gelu_value, gelu_slope


def grad_kernel(
    experts_ref, rows_hbm, slope_hbm, act_hbm, other_rows_hbm, first_hbm, second_hbm, blank_hbm,
    merged_hbm,
    rows_ref, slope_ref, act_ref, other_rows_ref, first_ref, second_ref, across_ref, grad_ref,
    load_sems, store_sems
):
    grp_index = lax.axis_index("grp")
    core = grp_index % 2
    base = lax.axis_index("ep") * EXP_COL
    owners = (
        experts_ref[0, grp_index] - base,
        experts_ref[0, grp_index + 1 - 2 * core] - base,
    )
    loads = [
        pltpu.make_async_copy(source, target, load_sems.at[k])
        for k, (source, target) in enumerate(
            (
                (rows_hbm, rows_ref),
                (slope_hbm, slope_ref),
                (act_hbm, act_ref),
                (other_rows_hbm, other_rows_ref),
                (first_hbm, first_ref),
                (second_hbm, second_ref),
            )
        )
    ]
    for load in loads:
        load.start()

    def store(n, k):
        copy = pltpu.make_async_copy(
            grad_ref.at[n, k], merged_hbm.at[:, k, owners[n]], store_sems.at[n, k]
        )
        copy.start()
        return copy

    def halves(n, source):
        for k in range(2):
            across_ref[n, k] = source[:, k * D : (k + 1) * D].T.reshape(Z, 2, FEAT, ROWS_SLOT)
        return [across_ref[n, k, :, core].reshape(D // 2, ROWS_SLOT) for k in range(2)]

    loads[0].wait()
    lefts = halves(0, rows_ref)
    stores = []
    for k, source in enumerate((slope_ref, act_ref)):
        loads[1 + k].wait()
        grad = jnp.dot(lefts[k], source[...], preferred_element_type=f32)
        grad_ref[0, k] = grad.astype(bf16).reshape(Z, FEAT, FF)
        stores.append(store(0, k))
    loads[3].wait()
    loads[4].wait()
    preact = jnp.dot(other_rows_ref[:, :D], first_ref[...], preferred_element_type=f32)
    loads[5].wait()
    hidden_grad = jnp.dot(other_rows_ref[:, D:], second_ref[...], preferred_element_type=f32)
    lefts = halves(1, other_rows_ref)
    gelu_value, gelu_slope = gelu_pair(preact)
    rights = ((hidden_grad * gelu_slope).astype(bf16), gelu_value.astype(bf16))
    same = owners[0] == owners[1]
    for k in (1, 0):
        grad = jnp.dot(lefts[k], rights[k], preferred_element_type=f32)
        held = jnp.where(same, grad_ref[0, k].reshape(D // 2, FF).astype(f32), 0.0)
        grad_ref[1, k] = (grad + held).astype(bf16).reshape(Z, FEAT, FF)
        stores[k].wait()
        stores.append(store(1, k))
    stores[2].wait()
    stores[3].wait()


def shape(dims, dtype=bf16):
    return jax.ShapeDtypeStruct(dims, dtype)


def whole():
    return pl.BlockSpec(memory_space=pltpu.VMEM)


def scalars():
    return pl.BlockSpec(memory_space=pltpu.SMEM)


def anywhere():
    return pl.BlockSpec(memory_space=pl.ANY)


def per_device(
    token_inputs,
    output_grads,
    gate_probs,
    token_slots,
    slot_experts,
    slot_capacity,
    weight_in,
    weight_out,
):
    ep_index = lax.axis_index("ep")
    grp_index = lax.axis_index("grp")
    place = jnp.stack([ep_index, grp_index]).astype(i32)
    slots = token_slots.reshape(EP * GRP, TOK)

    rows_out, pick = pl.pallas_call(
        send_kernel,
        in_specs=[anywhere()] * 4,
        out_specs=[anywhere(), whole()],
        out_shape=[shape((ROWS_MID, 2 * D)), shape((ROWS_MID, TOK))],
        scratch_shapes=[
            pltpu.VMEM((8, TOK), i32),
            pltpu.VMEM((TOK, D), bf16),
            pltpu.VMEM((TOK, D), bf16),
            pltpu.VMEM((1, TOK), f32),
            pltpu.VMEM((ROWS_MID, D), bf16),
            pltpu.VMEM((ROWS_MID, D), bf16),
            pltpu.SemaphoreType.DMA((6,)),
        ],
        name="send",
    )(slots, token_inputs, output_grads, gate_probs.reshape(1, TOK))
    rows_mid = lax.all_to_all(
        rows_out.reshape(GRP, CAP, 2 * D), "grp", split_axis=0, concat_axis=0, tiled=True
    ).reshape(ROWS_MID, 2 * D)

    forward, kept, blank = pl.pallas_call(
        route_kernel,
        grid_spec=pltpu.PrefetchScalarGridSpec(
            num_scalar_prefetch=1,
            grid=(1,),
            in_specs=[
                pl.BlockSpec((GRP, TOK), lambda i, p: (p[0], 0)),
                pl.BlockSpec((EP * GRP, TOK), lambda i, p: (0, 0)),
                pl.BlockSpec(memory_space=pltpu.SMEM),
            ],
            out_specs=[
                pl.BlockSpec((ROWS_SLOT, ROWS_MID), lambda i, p: (0, 0)),
                pl.BlockSpec((ROWS_SLOT, TOK), lambda i, p: (0, 0)),
                anywhere(),
            ],
            scratch_shapes=[
                pltpu.VMEM((ROWS_MID, TOK), f32),
                pltpu.VMEM((2, EXP_COL, FEAT, FF), bf16),
                pltpu.SemaphoreType.DMA((Z,)),
            ],
        ),
        out_shape=[
            shape((ROWS_SLOT, ROWS_MID)),
            shape((ROWS_SLOT, TOK), f32),
            shape((Z, 2, EXP_COL, FEAT, FF)),
        ],
        name="route",
    )(place, slots, slots, slot_capacity)

    first = weight_in.reshape(D, FF)
    second = weight_out.reshape(D, FF)
    early_first, early_second, _ = lax.optimization_barrier((first, second, forward))
    swap = [(g, g ^ 1) for g in range(GRP)]
    other_first = lax.ppermute(early_first, "grp", swap)
    other_second = lax.ppermute(early_second, "grp", swap)
    rows_mid, other_first, other_second, kept_rows = lax.optimization_barrier(
        (rows_mid, other_first, other_second, kept[:, 0] > 0.0)
    )
    rows_fwd = jnp.dot(forward, rows_mid, preferred_element_type=f32).astype(bf16)
    rows_slot = lax.all_to_all(
        rows_fwd.reshape(EP, CAP, 2 * D), "ep", split_axis=0, concat_axis=0, tiled=True
    ).reshape(ROWS_SLOT, 2 * D)

    rows_kept = jnp.where(kept_rows[:, None], rows_slot, jnp.zeros_like(rows_slot))
    other_rows = lax.ppermute(rows_kept, "grp", swap)
    preact = jnp.dot(rows_kept[:, :D], first, preferred_element_type=f32)
    gelu_value, gelu_slope = gelu_pair(preact)
    rows_later, other_rows = lax.optimization_barrier((rows_kept, other_rows))
    hidden_grad = jnp.dot(rows_later[:, D:], second, preferred_element_type=f32)
    preact_grad = (hidden_grad * gelu_slope).astype(bf16)
    merged = pl.pallas_call(
        grad_kernel,
        in_specs=[scalars()] + [anywhere()] * 7,
        out_specs=anywhere(),
        out_shape=shape((Z, 2, EXP_COL, FEAT, FF)),
        scratch_shapes=[
            pltpu.VMEM((ROWS_SLOT, 2 * D), bf16),
            pltpu.VMEM((ROWS_SLOT, FF), bf16),
            pltpu.VMEM((ROWS_SLOT, FF), bf16),
            pltpu.VMEM((ROWS_SLOT, 2 * D), bf16),
            pltpu.VMEM((D, FF), bf16),
            pltpu.VMEM((D, FF), bf16),
            pltpu.VMEM((2, 2, Z, 2, FEAT, ROWS_SLOT), bf16),
            pltpu.VMEM((2, 2, Z, FEAT, FF), bf16),
            pltpu.SemaphoreType.DMA((6,)),
            pltpu.SemaphoreType.DMA((2, 2)),
        ],
        input_output_aliases={7: 0},
        name="grad",
    )(
        slot_experts,
        rows_kept,
        preact_grad,
        gelu_value.astype(bf16),
        other_rows,
        other_first,
        other_second,
        blank,
    )
    back_rows = lax.dot_general(
        preact_grad, first, (((1,), (1,)), ((), ())), preferred_element_type=f32
    ).astype(bf16)
    expert_grads = lax.psum_scatter(
        merged.reshape(Z * 2 * EXP_COL * FEAT, FF),
        "grp",
        scatter_dimension=0,
        tiled=True,
        axis_index_groups=[[2 * z + c for z in range(Z)] for c in range(2)],
    ).reshape(2, EXP_COL, FEAT, FF)

    mid_back = lax.all_to_all(
        back_rows.reshape(EP, CAP, D), "ep", split_axis=0, concat_axis=0, tiled=True
    ).reshape(ROWS_SLOT, D)
    source_back = pl.pallas_call(
        back_kernel,
        in_specs=[whole(), whole()],
        out_specs=whole(),
        out_shape=shape((ROWS_MID, D)),
        name="back_mid",
    )(forward, mid_back)
    own_back = lax.all_to_all(
        source_back.reshape(GRP, CAP, D), "grp", split_axis=0, concat_axis=0, tiled=True
    ).reshape(ROWS_MID, D)
    input_grads = pl.pallas_call(
        back_kernel,
        in_specs=[whole(), whole()],
        out_specs=whole(),
        out_shape=shape((TOK, D)),
        name="back_own",
    )(pick, own_back)
    return input_grads, expert_grads


def solution(mesh):
    in_specs = (
        P(("ep", "grp"), None),
        P(("ep", "grp"), None),
        P(("ep", "grp")),
        P(),
        P("ep", None),
        P("ep", "grp"),
        P("ep", "grp", None, None),
        P("ep", "grp", None, None),
    )
    out_specs = (P(("ep", "grp"), None), P(None, "ep", "grp", None))
    return jax.shard_map(
        per_device, mesh=mesh, in_specs=in_specs, out_specs=out_specs, check_vma=False
    )
```
